32 devices in a mesh: conv: 4 (over y, core), seq: 4 (over z), tensor: 2 (over x).
Axes of the slice: x: 2, y: 2, z: 4, core: 2. Of those that a mesh axis runs over, the one named last changes fastest.
Arguments:
- queries: bfloat16 [4, 512, 4096], P('conv', 'seq', 'tensor'), may hold values from -6 to 6
- keys: bfloat16 [8, 1664, 1024], P('conv', ('seq', 'tensor')), may hold values from -6 to 6
- values: bfloat16 [8, 1664, 1024], P('conv', ('seq', 'tensor')), may hold values from -18 to 18
- q_gain: float32 [128], replicated, may hold values from 0.9 to 2.2
- k_gain: float32 [128], replicated, may hold values from 0.9 to 2.2
- gate: float32 [1], replicated, may hold values from 0.4 to 1.6
- tile_count: int32 [4], replicated, may hold values from 1 to 2, as said below
- tile_owner: int32 [4, 2], replicated, may hold values from -1 to 3, as said below
- visible: int32 [4, 512], replicated, may hold values from 0 to 2, as said below
- d_out: bfloat16 [4, 512, 4096], P('conv', 'seq', 'tensor'), may hold values from -12 to 12
Outputs:
- attended: bfloat16 [4, 512, 4096], P('conv', 'seq', 'tensor')
- d_queries: bfloat16 [4, 512, 4096], P('conv', 'seq', 'tensor')
- d_keys: bfloat16 [8, 1664, 1024], P('conv', ('seq', 'tensor'))
- d_values: bfloat16 [8, 1664, 1024], P('conv', ('seq', 'tensor'))
The draws below stay inside these ranges and needn't reach their ends.
Inputs may be any that keep to these rules, and one draw needn't show every extreme that they name: `tile_count`: some conversation has 2 tiles. `tile_owner`: entries with t at or past the conversation's count are -1. The tiles of one conversation have different owners, no two tiles share a slot, and some conv index holds 2 tiles. `visible`: never falls along a conversation's text; it is 0 at the first token and 2 at the last.
All inputs are finite; a program needn't handle non-finite values.
Results may differ from the reference program's by a relative error of at most 0.02.
Values may be sent and summed in bfloat16 or wider, within the bound.
A program may use at most 128 MiB of HBM per device.

```python
import math
import jax
import jax.numpy as jnp
from jax import lax

HD = 128
QHEADS = 32
KVHEADS = 8
MAXT = 2
TILE = 1601
TOK_SEQ = 128
GROUP = 4
TILE_PAD = 1664
LENGTH = 512
N_CONV = 4
N_SEQ = 4


def tile_plan(key):
    plan_key = jax.random.fold_in(key, 11)
    key_rows, key_cols, key_names, key_full, key_counts = jax.random.split(plan_key, 5)
    row_shift = jax.random.permutation(key_rows, N_CONV)
    col_shift = jax.random.permutation(key_cols, N_CONV)[:MAXT]
    relabel = jax.random.permutation(key_names, N_CONV)
    owners = relabel[(row_shift[:, None] + col_shift[None, :]) % N_CONV]
    full_owner = jax.random.randint(key_full, (), 0, N_CONV)
    tile_ids = jnp.arange(MAXT, dtype=jnp.int32)
    needed = jnp.max(jnp.where(owners == full_owner, tile_ids[None, :] + 1, 0), axis=1)
    counts = jnp.maximum(jax.random.randint(key_counts, (N_CONV,), 1, MAXT + 1), needed)
    owner_table = jnp.where(tile_ids[None, :] < counts[:, None], owners, -1)
    return (counts.astype(jnp.int32), owner_table.astype(jnp.int32))


def draw_tile_count(key, part):
    return tile_plan(key)[0]


def draw_tile_owner(key, part):
    return tile_plan(key)[1]


def draw_visible(key, part):
    thresholds = jax.random.randint(jax.random.fold_in(key, 23), (N_CONV, MAXT), 1, LENGTH)
    positions = jnp.arange(LENGTH, dtype=jnp.int32)
    return jnp.sum(thresholds[:, :, None] <= positions[None, None, :], axis=1).astype(jnp.int32)


def level_of(rng, dims, cuts, smallest, largest):
    loudness = 1.0
    for position, blocks in cuts:
        steps = jax.random.uniform(jax.random.fold_in(jax.random.fold_in(rng, 6), position), (blocks,), jnp.float32, smallest / len(cuts), largest / len(cuts))
        loudness = loudness * jnp.repeat(jnp.exp(steps), dims[position] // blocks).reshape((-1,) + (1,) * (len(dims) - 1 - position))
    return loudness


def centred(key, shape, deviation, limit, pieces=(), kind=jnp.bfloat16):
    values = jax.random.normal(key, shape, jnp.float32) * deviation
    if len(pieces) > 0:
        values = level_of(key, shape, pieces, -0.22, 0.18) * values
    return jnp.clip(values, min=-limit, max=limit).astype(kind)


def setup_inputs(seed: int = 0) -> dict:
    seeds = jax.random.split(jax.random.key(seed), 11)
    queries = centred(seeds[0], (N_CONV, LENGTH, QHEADS * HD), 1.0, 6.0, ((0, 4), (1, 4), (2, 2)))
    keys = centred(seeds[1], (N_CONV * MAXT, TILE_PAD, KVHEADS * HD), 1.0, 6.0, ((0, 4), (1, 8)))
    values = centred(seeds[2], (N_CONV * MAXT, TILE_PAD, KVHEADS * HD), 3.0, 18.0, ((0, 4), (1, 8)))
    q_gain = jnp.clip(jnp.exp(jax.random.uniform(seeds[3], (HD,), jnp.float32, math.log(0.9), math.log(2.2))), 0.9, 2.2)
    k_gain = jnp.clip(jnp.exp(jax.random.uniform(seeds[4], (HD,), jnp.float32, math.log(0.9), math.log(2.2))), 0.9, 2.2)
    gate = jnp.clip(jax.random.uniform(seeds[5], (1,), jnp.float32, 0.4, 1.6), 0.4, 1.6)
    tile_count = draw_tile_count(jax.random.fold_in(seeds[10], 71), 0)
    tile_owner = draw_tile_owner(jax.random.fold_in(seeds[10], 71), 0)
    visible = draw_visible(jax.random.fold_in(seeds[10], 71), 0)
    d_out = centred(seeds[9], (N_CONV, LENGTH, QHEADS * HD), 2.0, 12.0, ((0, 4), (1, 4), (2, 2)))
    return dict(queries=queries, keys=keys, values=values, q_gain=q_gain, k_gain=k_gain, gate=gate, tile_count=tile_count, tile_owner=tile_owner, visible=visible, d_out=d_out)


EPSILON = 1e-05

def head_norm(inputs, norm_gain):
    mean_square = lax.optimization_barrier(jnp.mean(inputs * inputs, axis=-1, keepdims=True))
    return inputs * lax.rsqrt(mean_square + EPSILON) * norm_gain

def rounded(inputs):
    return lax.optimization_barrier(inputs.astype(jnp.bfloat16)).astype(jnp.float32)

def reference(queries, keys, values, q_gain, k_gain, gate, tile_count, tile_owner, visible, d_out):
    score_scale = 1.0 / math.sqrt(HD)
    gate_value = jnp.tanh(gate[0])
    slots_all = N_CONV * MAXT
    key_raw = keys.astype(jnp.float32).reshape(slots_all, TILE_PAD, KVHEADS, HD)
    key_normed, key_back = jax.vjp(lambda inputs: head_norm(inputs, k_gain), key_raw)
    key_halfprec = key_normed.astype(jnp.bfloat16)
    value_all = values.reshape(slots_all, TILE_PAD, KVHEADS, HD)
    tile_ids = jnp.arange(MAXT, dtype=jnp.int32)
    row_ids = jnp.arange(TILE_PAD, dtype=jnp.int32)
    valid = tile_owner >= 0
    slot_index = jnp.where(valid, tile_owner * MAXT + tile_ids[None, :], 0).astype(jnp.int32)
    key_tile_ids = jnp.repeat(tile_ids, TILE_PAD)
    key_row_ids = jnp.tile(row_ids, MAXT)

    def one_conversation(conversation):
        chosen = slot_index[conversation]
        present = valid[conversation]
        tile_keys = jnp.where(present[:, None, None, None], key_halfprec[chosen], jnp.zeros((), jnp.bfloat16))
        tile_values = jnp.where(present[:, None, None, None], value_all[chosen], jnp.zeros((), jnp.bfloat16))
        flat_keys = tile_keys.reshape(MAXT * TILE_PAD, KVHEADS, HD).astype(jnp.float32)
        flat_values = tile_values.reshape(MAXT * TILE_PAD, KVHEADS, HD).astype(jnp.float32)
        seen_tiles = jnp.minimum(visible[conversation], tile_count[conversation])
        query_blocks = queries[conversation].astype(jnp.float32).reshape(N_SEQ, TOK_SEQ, QHEADS, HD)
        grad_blocks = d_out[conversation].astype(jnp.float32).reshape(N_SEQ, TOK_SEQ, KVHEADS, GROUP, HD)
        seen_blocks = seen_tiles.reshape(N_SEQ, TOK_SEQ)

        def one_block(carry, inputs):
            key_sum, value_sum = carry
            query_raw, cotangent, seen_here = inputs
            query_normed, query_back = jax.vjp(lambda vector: head_norm(vector, q_gain), query_raw)
            query_bf = rounded(query_normed).reshape(TOK_SEQ, KVHEADS, GROUP, HD)
            visible_keys = (key_tile_ids[None, :] < seen_here[:, None]) & (key_row_ids[None, :] < TILE)
            scores = jnp.einsum('pkgd,rkd->kgpr', query_bf, flat_keys) * score_scale
            weights = jnp.where(visible_keys[None, None], jnp.exp(scores), 0.0)
            weight_sum = lax.optimization_barrier(jnp.sum(weights, axis=-1))
            weighted = jnp.einsum('kgpr,rkd->pkgd', rounded(weights), flat_values)
            safe_sum = jnp.where(weight_sum > 0, weight_sum, 1.0)
            context = weighted / jnp.transpose(safe_sum, (2, 0, 1))[..., None]
            attended = (gate_value * context).astype(jnp.bfloat16).reshape(TOK_SEQ, QHEADS * HD)
            grad_ctx = rounded(gate_value * cotangent)
            row_delta = jnp.transpose(lax.optimization_barrier(jnp.sum(grad_ctx * context, axis=-1)), (1, 2, 0))
            probability = weights / safe_sum[..., None]
            grad_prob = jnp.einsum('pkgd,rkd->kgpr', grad_ctx, flat_values)
            grad_score = rounded(probability * (grad_prob - row_delta[..., None]))
            grad_query = jnp.einsum('kgpr,rkd->pkgd', grad_score, flat_keys) * score_scale
            query_grad = query_back(grad_query.reshape(TOK_SEQ, QHEADS, HD))[0]
            query_grad = query_grad.astype(jnp.bfloat16).reshape(TOK_SEQ, QHEADS * HD)
            key_part = jnp.einsum('kgpr,pkgd->rkd', grad_score, query_bf) * score_scale
            value_part = jnp.einsum('kgpr,pkgd->rkd', rounded(probability), grad_ctx)
            key_sum = key_sum + rounded(key_part)
            value_sum = value_sum + rounded(value_part)
            return ((key_sum, value_sum), (attended, query_grad))
        zero_grads = jnp.zeros((MAXT * TILE_PAD, KVHEADS, HD), jnp.float32)
        (key_sum, value_sum), (attended, query_grad) = lax.scan(one_block, (zero_grads, zero_grads), (query_blocks, grad_blocks, seen_blocks))
        key_grad = key_sum.astype(jnp.bfloat16).reshape(MAXT, TILE_PAD, KVHEADS, HD)
        value_grad = value_sum.astype(jnp.bfloat16).reshape(MAXT, TILE_PAD, KVHEADS, HD)
        return (attended.reshape(LENGTH, QHEADS * HD), query_grad.reshape(LENGTH, QHEADS * HD), key_grad, value_grad)
    attended, d_queries, key_grad, value_grad = lax.map(one_conversation, jnp.arange(N_CONV, dtype=jnp.int32))
    target = jnp.where(valid, tile_owner * MAXT + tile_ids[None, :], slots_all).astype(jnp.int32).reshape(-1)
    positioned_keys = jnp.zeros((slots_all, TILE_PAD, KVHEADS, HD), jnp.float32)
    positioned_keys = positioned_keys.at[target].add(key_grad.reshape(slots_all, TILE_PAD, KVHEADS, HD).astype(jnp.float32), mode='drop')
    placed_values = jnp.zeros((slots_all, TILE_PAD, KVHEADS, HD), jnp.float32)
    placed_values = placed_values.at[target].add(value_grad.reshape(slots_all, TILE_PAD, KVHEADS, HD).astype(jnp.float32), mode='drop')
    d_keys = key_back(positioned_keys)[0].astype(jnp.bfloat16).reshape(slots_all, TILE_PAD, KVHEADS * HD)
    d_values = placed_values.astype(jnp.bfloat16).reshape(slots_all, TILE_PAD, KVHEADS * HD)
    return (attended, d_queries, d_keys, d_values)
```

```python
from functools import partial
import math

import jax
import jax.numpy as jnp
from jax import lax
from jax.experimental import pallas as pl
from jax.experimental.pallas import tpu as pltpu
from jax.sharding import PartitionSpec as P

TILE = 1601


EPSILON = 1e-05


def head_norm(inputs, norm_gain):
    mean_square = jnp.mean(inputs * inputs, axis=-1, keepdims=True)
    return inputs * lax.rsqrt(mean_square + EPSILON) * norm_gain


def key_mask(seen_tiles, tile_index, row_start, row_count):
    row_ids = row_start + jnp.arange(row_count, dtype=jnp.int32)
    return (seen_tiles > tile_index)[:, None] & (row_ids < TILE)[None, :]


def tile_weights(query_bf, key_tile, visible_keys, score_scale):
    scores = (
        jnp.einsum("pkgd,rkd->kgpr", query_bf, key_tile, preferred_element_type=jnp.float32)
        * score_scale
    )
    return jnp.where(visible_keys[None, None], jnp.exp(scores), 0.0)


def tile_forward(query_bf, key_tile, value_tile, visible_keys, score_scale):
    weights = tile_weights(query_bf, key_tile, visible_keys, score_scale)
    weighted = jnp.einsum(
        "kgpr,rkd->pkgd",
        weights.astype(jnp.bfloat16),
        value_tile,
        preferred_element_type=jnp.float32,
    )
    return (jnp.sum(weights, axis=-1), weighted)


def tile_gradients(
    query_bf,
    grad_bf,
    key_tile,
    value_tile,
    visible_keys,
    safe_sum,
    row_delta,
    score_scale,
    block_count,
):
    weights = tile_weights(query_bf, key_tile, visible_keys, score_scale)
    probability = weights / safe_sum[..., None]
    grad_prob = jnp.einsum(
        "pkgd,rkd->kgpr", grad_bf, value_tile, preferred_element_type=jnp.float32
    )
    grad_score = (probability * (grad_prob - row_delta[..., None])).astype(jnp.bfloat16)
    prob_bf = probability.astype(jnp.bfloat16)
    grad_query = (
        jnp.einsum("kgpr,rkd->pkgd", grad_score, key_tile, preferred_element_type=jnp.float32)
        * score_scale
    )
    kv_local, group_size, token_count, row_count = grad_score.shape
    head_size = query_bf.shape[-1]
    block_tokens = token_count // block_count
    score_blocks = grad_score.reshape(kv_local, group_size, block_count, block_tokens, row_count)
    prob_blocks = prob_bf.reshape(kv_local, group_size, block_count, block_tokens, row_count)
    query_blocks = query_bf.reshape(block_count, block_tokens, kv_local, group_size, head_size)
    grad_blocks = grad_bf.reshape(block_count, block_tokens, kv_local, group_size, head_size)
    key_part = (
        jnp.einsum(
            "kgbpr,bpkgd->brkd", score_blocks, query_blocks, preferred_element_type=jnp.float32
        )
        * score_scale
    )
    value_part = jnp.einsum(
        "kgbpr,bpkgd->brkd", prob_blocks, grad_blocks, preferred_element_type=jnp.float32
    )
    key_part = jnp.sum(
        lax.optimization_barrier(key_part.astype(jnp.bfloat16)).astype(jnp.float32), axis=0
    )
    value_part = jnp.sum(
        lax.optimization_barrier(value_part.astype(jnp.bfloat16)).astype(jnp.float32), axis=0
    )
    return (
        grad_query,
        key_part.reshape(row_count, kv_local * head_size),
        value_part.reshape(row_count, kv_local * head_size),
    )


def attend_forward(query_bf, tile_keys, tile_values, seen_tiles, row_start, score_scale):
    row_count, slot_count, features = tile_keys.shape
    token_count, kv_local, group_size, head_size = query_bf.shape
    weight_sum = jnp.zeros((kv_local, group_size, token_count), jnp.float32)
    weighted = jnp.zeros(query_bf.shape, jnp.float32)
    for tile_index in range(slot_count):
        key_tile = tile_keys[:, tile_index].reshape(row_count, kv_local, head_size)
        value_tile = tile_values[:, tile_index].reshape(row_count, kv_local, head_size)
        visible_keys = key_mask(seen_tiles, tile_index, row_start, row_count)
        work = partial(tile_forward, query_bf, key_tile, value_tile, visible_keys, score_scale)
        part_sum, part_weighted = work()
        weight_sum = weight_sum + part_sum
        weighted = weighted + part_weighted
    return (weight_sum, weighted)


def attend_backward(
    query_bf,
    grad_bf,
    tile_keys,
    tile_values,
    seen_tiles,
    row_start,
    safe_sum,
    row_delta,
    score_scale,
    block_tokens,
):
    row_count, slot_count, features = tile_keys.shape
    token_count, kv_local, group_size, head_size = query_bf.shape
    block_count = token_count // block_tokens
    grad_query = jnp.zeros(query_bf.shape, jnp.float32)
    key_parts = []
    value_parts = []
    for tile_index in range(slot_count):
        key_tile = tile_keys[:, tile_index].reshape(row_count, kv_local, head_size)
        value_tile = tile_values[:, tile_index].reshape(row_count, kv_local, head_size)
        visible_keys = key_mask(seen_tiles, tile_index, row_start, row_count)
        work = partial(
            tile_gradients,
            query_bf,
            grad_bf,
            key_tile,
            value_tile,
            visible_keys,
            safe_sum,
            row_delta,
            score_scale,
            block_count,
        )
        part_query, key_part, value_part = work()
        grad_query = grad_query + part_query
        key_parts.append(key_part)
        value_parts.append(value_part)
    return (grad_query, jnp.stack(key_parts, axis=1), jnp.stack(value_parts, axis=1))


def row_shards(queries, keys, values, q_gain, k_gain, gate, tile_count, tile_owner, visible, d_out):
    conv_count = lax.axis_size("conv")
    tensor_count = lax.axis_size("tensor")
    conv_index = lax.axis_index("conv")
    sequence_index = lax.axis_index("seq")
    slot_count, row_local, features = keys.shape
    head_size = q_gain.shape[0]
    kv_heads = features // head_size
    kv_local = kv_heads // tensor_count
    token_count = queries.shape[1]
    query_heads = queries.shape[2] // head_size
    group_size = query_heads // kv_local
    score_scale = 1.0 / math.sqrt(head_size)
    gate_value = jnp.tanh(gate[0])
    conv_ids = jnp.arange(conv_count, dtype=jnp.int32)
    transfers = (tile_owner == conv_index).astype(jnp.bfloat16)
    own_owners = lax.dynamic_index_in_dim(tile_owner, conv_index, 0, keepdims=False)
    takes = (own_owners[:, None] == conv_ids[None, :]).astype(jnp.bfloat16)
    own_count = lax.dynamic_index_in_dim(tile_count, conv_index, 0, keepdims=False)
    seen_all = jnp.minimum(
        lax.dynamic_index_in_dim(visible, conv_index, 0, keepdims=False), own_count
    )
    key_raw = keys.astype(jnp.float32).reshape(slot_count, row_local, kv_heads, head_size)
    key_normed, key_back = jax.vjp(lambda inputs: head_norm(inputs, k_gain), key_raw)
    key_halfprec = key_normed.astype(jnp.bfloat16).reshape(slot_count, row_local, features)
    outgoing_keys = jnp.einsum(
        "wn,nki->wki", transfers, key_halfprec, preferred_element_type=jnp.float32
    ).astype(jnp.bfloat16)
    send_values = jnp.einsum(
        "wn,nki->wki", transfers, values, preferred_element_type=jnp.float32
    ).astype(jnp.bfloat16)
    got_keys, got_values = (
        lax.all_to_all(
            lax.all_to_all(outgoing_keys, "conv", split_axis=0, concat_axis=0, tiled=True),
            "tensor",
            split_axis=2,
            concat_axis=1,
            tiled=True,
        ),
        lax.all_to_all(
            lax.all_to_all(send_values, "conv", split_axis=0, concat_axis=0, tiled=True),
            "tensor",
            split_axis=2,
            concat_axis=1,
            tiled=True,
        ),
    )
    tile_keys = jnp.einsum(
        "to,orf->rtf", takes, got_keys, preferred_element_type=jnp.float32
    ).astype(jnp.bfloat16)
    tile_values = jnp.einsum(
        "to,orf->rtf", takes, got_values, preferred_element_type=jnp.float32
    ).astype(jnp.bfloat16)
    query_raw = queries[0].astype(jnp.float32).reshape(token_count, query_heads, head_size)
    query_normed, query_back = jax.vjp(lambda inputs: head_norm(inputs, q_gain), query_raw)
    query_bf = query_normed.astype(jnp.bfloat16).reshape(
        token_count, kv_local, group_size, head_size
    )
    grad_bf = (
        (gate_value * d_out[0].astype(jnp.float32))
        .astype(jnp.bfloat16)
        .reshape(token_count, kv_local, group_size, head_size)
    )
    own_start = sequence_index * token_count
    all_queries = lax.all_gather(query_bf, "seq", axis=0, tiled=True)
    all_grads = lax.all_gather(grad_bf, "seq", axis=0, tiled=True)
    share_rows = tile_keys.shape[0]
    row_start = sequence_index * share_rows
    part_sum, part_weighted = attend_forward(
        all_queries, tile_keys, tile_values, seen_all, row_start, score_scale
    )
    all_weighted, all_weight_sum = (
        lax.psum(part_weighted.astype(jnp.bfloat16), "seq").astype(jnp.float32),
        lax.psum(part_sum.astype(jnp.bfloat16), "seq").astype(jnp.float32),
    )
    safe_all = jnp.where(all_weight_sum > 0, all_weight_sum, 1.0)
    context_all = all_weighted / jnp.transpose(safe_all, (2, 0, 1))[..., None]
    context = lax.dynamic_slice_in_dim(context_all, own_start, token_count, 0)
    row_delta = jnp.transpose(
        jnp.sum(all_grads.astype(jnp.float32) * context_all, axis=-1), (1, 2, 0)
    )
    grad_part, key_sums, value_sums = attend_backward(
        all_queries,
        all_grads,
        tile_keys,
        tile_values,
        seen_all,
        row_start,
        safe_all,
        row_delta,
        score_scale,
        token_count,
    )
    grad_query = lax.psum_scatter(
        grad_part.astype(jnp.bfloat16), "seq", scatter_dimension=0, tiled=True
    ).astype(jnp.float32)
    attended = (
        (gate_value * context).astype(jnp.bfloat16).reshape(1, token_count, query_heads * head_size)
    )
    key_round = key_sums.astype(jnp.bfloat16)
    value_round = value_sums.astype(jnp.bfloat16)
    back_keys = jnp.einsum(
        "to,rtf->orf", takes, key_round, preferred_element_type=jnp.float32
    ).astype(jnp.bfloat16)
    back_values = jnp.einsum(
        "to,rtf->orf", takes, value_round, preferred_element_type=jnp.float32
    ).astype(jnp.bfloat16)
    returned_keys, returned_values = (
        lax.all_to_all(
            lax.all_to_all(back_keys, "conv", split_axis=0, concat_axis=0, tiled=True),
            "tensor",
            split_axis=1,
            concat_axis=2,
            tiled=True,
        ),
        lax.all_to_all(
            lax.all_to_all(back_values, "conv", split_axis=0, concat_axis=0, tiled=True),
            "tensor",
            split_axis=1,
            concat_axis=2,
            tiled=True,
        ),
    )
    positioned_keys = jnp.einsum(
        "ew,eig->wig", transfers, returned_keys, preferred_element_type=jnp.float32
    )
    d_values = jnp.einsum(
        "ew,eig->wig", transfers, returned_values, preferred_element_type=jnp.float32
    ).astype(jnp.bfloat16)
    d_keys = key_back(positioned_keys.reshape(slot_count, row_local, kv_heads, head_size))[0]
    d_keys = d_keys.astype(jnp.bfloat16).reshape(slot_count, row_local, features)
    d_queries = query_back(grad_query.reshape(token_count, query_heads, head_size))[0]
    d_queries = d_queries.astype(jnp.bfloat16).reshape(1, token_count, query_heads * head_size)
    return (attended, d_queries, d_keys, d_values)


LOG2E = math.log2(math.e)


def row_chunks(rows):
    starts = list(range(0, max(rows - 511, 1), 512))
    return [(a, b - a) for a, b in zip(starts, starts[1:] + [rows])]


def inverse_rms(inputs):
    return lax.rsqrt(jnp.mean(inputs * inputs, axis=-1, keepdims=True) + EPSILON)


def norm_back(inputs, inv, gained):
    return inv * gained - inputs * (inv * inv * inv) * jnp.mean(
        inputs * gained, axis=-1, keepdims=True
    )


def dot(lhs, rhs):
    return jnp.dot(lhs, rhs, preferred_element_type=jnp.float32)


def prepare_tile(tile, k_raw, v_raw, k_gain, kn, kt, vt):
    rows = k_raw.shape[1]
    for start in range(0, rows, 128):
        at = pl.ds(start, 128)
        raw = k_raw[tile, at, :].astype(jnp.float32)
        normed = raw * inverse_rms(raw) * k_gain
        kn[tile, at, :] = normed.astype(jnp.bfloat16)
        kt[tile, :, at] = normed.T.astype(jnp.bfloat16)
        vt[tile, :, at] = v_raw[tile, at, :].astype(jnp.float32).T.astype(jnp.bfloat16)


def finish_tile(tile, k_raw, k_gain, dk, dv, dk_out, dv_out):
    rows = k_raw.shape[1]
    for start in range(0, rows, 128):
        at = pl.ds(start, 128)
        raw = k_raw[tile, at, :].astype(jnp.float32)
        grad = dk[tile, at, :] * (1.0 / LOG2E) * k_gain
        dk_out[tile, at, :] = norm_back(raw, inverse_rms(raw), grad).astype(jnp.bfloat16)
        dv_out[tile, at, :] = dv[tile, at, :].astype(jnp.bfloat16)


def attend_block(
    block, last_seen, tiles, q_raw, d_out, seen, gate_value, q_gain, v_raw, kn, kt, vt,
    att_out, dq_out, wts, qs, qst, dos, dost, acc, total, dqt, dk, dv,
):
    size = q_gain.shape[1]
    group = q_raw.shape[1] // size
    count = seen.shape[2] // group
    rows = v_raw.shape[1]
    chunks = row_chunks(rows)
    scale = 1.0 / math.sqrt(size)
    at = pl.ds(pl.multiple_of(block * count, count), count)
    for g in range(group):
        raw = q_raw[at, pl.ds(g * size, size)].astype(jnp.float32)
        normed = raw * inverse_rms(raw) * (q_gain * (scale * LOG2E))
        qs[pl.ds(g * count, count), :] = normed.astype(jnp.bfloat16)
        qst[:, pl.ds(g * count, count)] = normed.T.astype(jnp.bfloat16)
    seen_row = seen[block]
    acc[...] = jnp.zeros_like(acc)
    total[...] = jnp.zeros_like(total)
    dqt[...] = jnp.zeros_like(dqt)

    for tile in range(tiles):
        @pl.when(last_seen > tile)
        def _(tile=tile):
            mask = (seen_row > tile).astype(jnp.float32)
            part = jnp.zeros(acc.shape, jnp.float32)
            part_sum = jnp.zeros(total.shape, jnp.float32)
            for start, length in chunks:
                here = pl.ds(start, length)
                w = jnp.exp2(dot(kn[tile, here, :], qst[...]))
                if start + length > TILE:
                    ids = start + lax.broadcasted_iota(jnp.int32, w.shape, 0)
                    w = jnp.where(ids < TILE, w, 0.0)
                part_sum = part_sum + jnp.sum(w, axis=0, keepdims=True)
                w_bf = w.astype(jnp.bfloat16)
                wts[tile, here, :] = w_bf
                part = part + dot(vt[tile, :, here], w_bf)
            acc[...] += part * mask
            total[...] += part_sum * mask

    safe = jnp.where(total[...] > 0, total[...], 1.0)
    inv = 1.0 / safe
    ctx = acc[...] * inv
    for g in range(group):
        lanes = pl.ds(g * count, count)
        grad = d_out[at, pl.ds(g * size, size)].astype(jnp.float32) * gate_value
        dost[:, lanes] = grad.T
        att_out[at, pl.ds(g * size, size)] = (
            (gate_value * ctx[:, g * count:(g + 1) * count]).T.astype(jnp.bfloat16)
        )
    scaled = (dost[...] * inv).astype(jnp.bfloat16)
    scaled32 = scaled.astype(jnp.float32)
    delta = jnp.sum(scaled32 * ctx, axis=0, keepdims=True)

    for tile in range(tiles):
        @pl.when(last_seen > tile)
        def _(tile=tile):
            mask = (seen_row > tile).astype(jnp.float32)
            cut32 = scaled32 * mask
            cut = cut32.astype(jnp.bfloat16)
            for g in range(group):
                dos[pl.ds(g * count, count), :] = (
                    cut32[:, g * count:(g + 1) * count].T.astype(jnp.bfloat16)
                )
            low = delta * mask
            part = jnp.zeros(dqt.shape, jnp.float32)
            for start, length in chunks:
                here = pl.ds(start, length)
                w_bf = wts[tile, here, :]
                dp = dot(v_raw[tile, here, :], cut)
                ds = (w_bf.astype(jnp.float32) * (dp - low)).astype(jnp.bfloat16)
                dv[tile, here, :] += dot(w_bf, dos[...])
                dk[tile, here, :] += dot(ds, qs[...])
                part = part + dot(kt[tile, :, here], ds)
            dqt[...] += part

    for g in range(group):
        raw = q_raw[at, pl.ds(g * size, size)].astype(jnp.float32)
        grad = dqt[:, pl.ds(g * count, count)].T * (q_gain * scale)
        dq_out[at, pl.ds(g * size, size)] = norm_back(raw, inverse_rms(raw), grad).astype(
            jnp.bfloat16
        )


def head_kernel(
    last, counts, gate, q_raw, d_out, k_raw, v_raw, seen, q_gain_ref, k_gain_ref,
    att_out, dq_out, dk_out, dv_out,
    kn, kt, vt, wts, qs, qst, dos, dost, acc, total, dqt, dk, dv,
):
    tiles = k_raw.shape[0]
    q_gain = q_gain_ref[...]
    k_gain = k_gain_ref[...]
    dk[...] = jnp.zeros_like(dk)
    dv[...] = jnp.zeros_like(dv)
    for tile in range(tiles):
        prepare_tile(tile, k_raw, v_raw, k_gain, kn, kt, vt)

    @pl.loop(0, seen.shape[0])
    def _(block):
        attend_block(
            block, last[block], tiles, q_raw, d_out, seen, gate[0], q_gain, v_raw, kn, kt, vt,
            att_out, dq_out, wts, qs, qst, dos, dost, acc, total, dqt, dk, dv,
        )

    for tile in range(tiles):
        finish_tile(tile, k_raw, k_gain, dk, dv, dk_out, dv_out)


def core_scratch(tiles, rows, size, lanes):
    bf, f32 = jnp.bfloat16, jnp.float32
    return [
        pltpu.VMEM((tiles, rows, size), bf),
        pltpu.VMEM((tiles, size, rows), bf),
        pltpu.VMEM((tiles, size, rows), bf),
        pltpu.VMEM((tiles, rows, lanes), bf),
        pltpu.VMEM((lanes, size), bf),
        pltpu.VMEM((size, lanes), bf),
        pltpu.VMEM((lanes, size), bf),
        pltpu.VMEM((size, lanes), f32),
        pltpu.VMEM((size, lanes), f32),
        pltpu.VMEM((1, lanes), f32),
        pltpu.VMEM((size, lanes), f32),
        pltpu.VMEM((tiles, rows, size), f32),
        pltpu.VMEM((tiles, rows, size), f32),
    ]


def head_shards(queries, keys, values, q_gain, k_gain, gate, tile_count, tile_owner, visible, d_out):
    conv_count = lax.axis_size("conv")
    tensor_count = lax.axis_size("tensor")
    seq_count = lax.axis_size("seq")
    conv_index = lax.axis_index("conv")
    slot_count, row_local, features = keys.shape
    size = q_gain.shape[0]
    block_tokens, width = queries.shape[1:]
    group = width // (features // tensor_count)
    lanes = group * block_tokens
    everyone = ("conv", "seq", "tensor")

    own_owners = lax.dynamic_index_in_dim(tile_owner, conv_index, 0, keepdims=False)
    own_count = lax.dynamic_index_in_dim(tile_count, conv_index, 0, keepdims=False)
    seen = jnp.minimum(lax.dynamic_index_in_dim(visible, conv_index, 0, keepdims=False), own_count)
    seen = seen.reshape(seq_count, 1, block_tokens)
    last = seen[:, 0, -1]
    seen = jnp.tile(seen, (1, 1, group))

    both = jnp.stack([queries[0], d_out[0]]).reshape(2, block_tokens, seq_count, width // seq_count)
    both = lax.all_to_all(both, "seq", split_axis=2, concat_axis=1, tiled=True)
    both = both.reshape(2, seq_count * block_tokens, width // seq_count)

    goes = tile_owner == conv_index
    slot_of = jnp.argmax(goes, axis=1)
    pair = jnp.stack([keys, values], axis=2).reshape(
        slot_count, row_local, 2, tensor_count, seq_count, size
    )
    pair = jnp.transpose(pair, (0, 4, 3, 1, 2, 5))
    sent = jnp.take(pair, slot_of, axis=0).reshape(-1, row_local, 2, size)
    got = lax.all_to_all(sent, everyone, split_axis=0, concat_axis=0, tiled=True)
    got = got.reshape(conv_count, -1, 2, size)
    mine = jnp.take(got, jnp.maximum(own_owners, 0), axis=0)
    rows = mine.shape[1]

    vmem = pl.BlockSpec(memory_space=pltpu.VMEM)
    smem = pl.BlockSpec(memory_space=pltpu.SMEM)
    att, dq, dk, dv = pl.pallas_call(
        head_kernel,
        out_shape=[jax.ShapeDtypeStruct(both.shape[1:], jnp.bfloat16)] * 2
        + [jax.ShapeDtypeStruct((slot_count, rows, size), jnp.bfloat16)] * 2,
        in_specs=[smem] * 3 + [vmem] * 7,
        out_specs=[vmem] * 4,
        scratch_shapes=core_scratch(slot_count, rows, size, lanes),
        compiler_params=pltpu.CompilerParams(vmem_limit_bytes=60 << 20),
    )(
        last, own_count.reshape(1), jnp.tanh(gate), both[0], both[1], mine[:, :, 0], mine[:, :, 1],
        seen, q_gain[None], k_gain[None],
    )

    outs = jnp.stack([att, dq]).reshape(2, seq_count, block_tokens, width // seq_count)
    outs = lax.all_to_all(outs, "seq", split_axis=1, concat_axis=3, tiled=True)
    attended = outs[0].reshape(1, block_tokens, width)
    d_queries = outs[1].reshape(1, block_tokens, width)

    tile_of = jnp.argmax(own_owners[None, :] == jnp.arange(conv_count)[:, None], axis=1)
    back = jnp.take(jnp.stack([dk, dv], axis=1), tile_of, axis=0)
    back = back.reshape(conv_count, 2, -1, row_local, size)
    back = jnp.transpose(back, (0, 2, 1, 3, 4)).reshape(-1, 2, row_local, size)
    back = lax.all_to_all(back, everyone, split_axis=0, concat_axis=0, tiled=True)
    back = back.reshape(conv_count, seq_count, tensor_count, 2, row_local, size)
    taker = jnp.argmax(goes, axis=0)
    used = jnp.any(goes, axis=0)
    back = jnp.take(back, taker, axis=0)
    back = jnp.transpose(back, (3, 0, 4, 2, 1, 5)).reshape(2, slot_count, row_local, features)
    back = jnp.where(used[None, :, None, None], back, jnp.zeros((), jnp.bfloat16))
    return (attended, d_queries, back[0], back[1])


def shards(queries, keys, *rest):
    heads = keys.shape[2] // rest[1].shape[0]
    split = lax.axis_size("seq") * lax.axis_size("tensor")
    return (head_shards if heads == split else row_shards)(queries, keys, *rest)


def solution(mesh):
    in_specs = (
        P("conv", "seq", "tensor"),
        P("conv", ("seq", "tensor"), None),
        P("conv", ("seq", "tensor"), None),
        P(),
        P(),
        P(),
        P(),
        P(),
        P(),
        P("conv", "seq", "tensor"),
    )
    out_specs = (
        P("conv", "seq", "tensor"),
        P("conv", "seq", "tensor"),
        P("conv", ("seq", "tensor"), None),
        P("conv", ("seq", "tensor"), None),
    )
    return jax.shard_map(shards, mesh=mesh, in_specs=in_specs, out_specs=out_specs, check_vma=False)
```

```python
from functools import partial
import math

import jax
import jax.numpy as jnp
from jax import lax
from jax.experimental import pallas as pl
from jax.experimental.pallas import tpu as pltpu
from jax.sharding import PartitionSpec as P

TILE = 1601


EPSILON = 1e-05


def head_norm(inputs, norm_gain):
    mean_square = jnp.mean(inputs * inputs, axis=-1, keepdims=True)
    return inputs * lax.rsqrt(mean_square + EPSILON) * norm_gain


def key_mask(seen_tiles, tile_index, row_start, row_count):
    row_ids = row_start + jnp.arange(row_count, dtype=jnp.int32)
    return (seen_tiles > tile_index)[:, None] & (row_ids < TILE)[None, :]


def tile_weights(query_bf, key_tile, visible_keys, score_scale):
    scores = (
        jnp.einsum("pkgd,rkd->kgpr", query_bf, key_tile, preferred_element_type=jnp.float32)
        * score_scale
    )
    return jnp.where(visible_keys[None, None], jnp.exp(scores), 0.0)


def tile_forward(query_bf, key_tile, value_tile, visible_keys, score_scale):
    weights = tile_weights(query_bf, key_tile, visible_keys, score_scale)
    weighted = jnp.einsum(
        "kgpr,rkd->pkgd",
        weights.astype(jnp.bfloat16),
        value_tile,
        preferred_element_type=jnp.float32,
    )
    return (jnp.sum(weights, axis=-1), weighted)


def tile_gradients(
    query_bf,
    grad_bf,
    key_tile,
    value_tile,
    visible_keys,
    safe_sum,
    row_delta,
    score_scale,
    block_count,
):
    weights = tile_weights(query_bf, key_tile, visible_keys, score_scale)
    probability = weights / safe_sum[..., None]
    grad_prob = jnp.einsum(
        "pkgd,rkd->kgpr", grad_bf, value_tile, preferred_element_type=jnp.float32
    )
    grad_score = (probability * (grad_prob - row_delta[..., None])).astype(jnp.bfloat16)
    prob_bf = probability.astype(jnp.bfloat16)
    grad_query = (
        jnp.einsum("kgpr,rkd->pkgd", grad_score, key_tile, preferred_element_type=jnp.float32)
        * score_scale
    )
    kv_local, group_size, token_count, row_count = grad_score.shape
    head_size = query_bf.shape[-1]
    block_tokens = token_count // block_count
    score_blocks = grad_score.reshape(kv_local, group_size, block_count, block_tokens, row_count)
    prob_blocks = prob_bf.reshape(kv_local, group_size, block_count, block_tokens, row_count)
    query_blocks = query_bf.reshape(block_count, block_tokens, kv_local, group_size, head_size)
    grad_blocks = grad_bf.reshape(block_count, block_tokens, kv_local, group_size, head_size)
    key_part = (
        jnp.einsum(
            "kgbpr,bpkgd->brkd", score_blocks, query_blocks, preferred_element_type=jnp.float32
        )
        * score_scale
    )
    value_part = jnp.einsum(
        "kgbpr,bpkgd->brkd", prob_blocks, grad_blocks, preferred_element_type=jnp.float32
    )
    key_part = jnp.sum(
        lax.optimization_barrier(key_part.astype(jnp.bfloat16)).astype(jnp.float32), axis=0
    )
    value_part = jnp.sum(
        lax.optimization_barrier(value_part.astype(jnp.bfloat16)).astype(jnp.float32), axis=0
    )
    return (
        grad_query,
        key_part.reshape(row_count, kv_local * head_size),
        value_part.reshape(row_count, kv_local * head_size),
    )


def attend_forward(query_bf, tile_keys, tile_values, seen_tiles, row_start, score_scale):
    row_count, slot_count, features = tile_keys.shape
    token_count, kv_local, group_size, head_size = query_bf.shape
    weight_sum = jnp.zeros((kv_local, group_size, token_count), jnp.float32)
    weighted = jnp.zeros(query_bf.shape, jnp.float32)
    for tile_index in range(slot_count):
        key_tile = tile_keys[:, tile_index].reshape(row_count, kv_local, head_size)
        value_tile = tile_values[:, tile_index].reshape(row_count, kv_local, head_size)
        visible_keys = key_mask(seen_tiles, tile_index, row_start, row_count)
        work = partial(tile_forward, query_bf, key_tile, value_tile, visible_keys, score_scale)
        part_sum, part_weighted = work()
        weight_sum = weight_sum + part_sum
        weighted = weighted + part_weighted
    return (weight_sum, weighted)


def attend_backward(
    query_bf,
    grad_bf,
    tile_keys,
    tile_values,
    seen_tiles,
    row_start,
    safe_sum,
    row_delta,
    score_scale,
    block_tokens,
):
    row_count, slot_count, features = tile_keys.shape
    token_count, kv_local, group_size, head_size = query_bf.shape
    block_count = token_count // block_tokens
    grad_query = jnp.zeros(query_bf.shape, jnp.float32)
    key_parts = []
    value_parts = []
    for tile_index in range(slot_count):
        key_tile = tile_keys[:, tile_index].reshape(row_count, kv_local, head_size)
        value_tile = tile_values[:, tile_index].reshape(row_count, kv_local, head_size)
        visible_keys = key_mask(seen_tiles, tile_index, row_start, row_count)
        work = partial(
            tile_gradients,
            query_bf,
            grad_bf,
            key_tile,
            value_tile,
            visible_keys,
            safe_sum,
            row_delta,
            score_scale,
            block_count,
        )
        part_query, key_part, value_part = work()
        grad_query = grad_query + part_query
        key_parts.append(key_part)
        value_parts.append(value_part)
    return (grad_query, jnp.stack(key_parts, axis=1), jnp.stack(value_parts, axis=1))


def row_shards(queries, keys, values, q_gain, k_gain, gate, tile_count, tile_owner, visible, d_out):
    conv_count = lax.axis_size("conv")
    tensor_count = lax.axis_size("tensor")
    conv_index = lax.axis_index("conv")
    sequence_index = lax.axis_index("seq")
    slot_count, row_local, features = keys.shape
    head_size = q_gain.shape[0]
    kv_heads = features // head_size
    kv_local = kv_heads // tensor_count
    token_count = queries.shape[1]
    query_heads = queries.shape[2] // head_size
    group_size = query_heads // kv_local
    score_scale = 1.0 / math.sqrt(head_size)
    gate_value = jnp.tanh(gate[0])
    conv_ids = jnp.arange(conv_count, dtype=jnp.int32)
    transfers = (tile_owner == conv_index).astype(jnp.bfloat16)
    own_owners = lax.dynamic_index_in_dim(tile_owner, conv_index, 0, keepdims=False)
    takes = (own_owners[:, None] == conv_ids[None, :]).astype(jnp.bfloat16)
    own_count = lax.dynamic_index_in_dim(tile_count, conv_index, 0, keepdims=False)
    seen_all = jnp.minimum(
        lax.dynamic_index_in_dim(visible, conv_index, 0, keepdims=False), own_count
    )
    key_raw = keys.astype(jnp.float32).reshape(slot_count, row_local, kv_heads, head_size)
    key_normed, key_back = jax.vjp(lambda inputs: head_norm(inputs, k_gain), key_raw)
    key_halfprec = key_normed.astype(jnp.bfloat16).reshape(slot_count, row_local, features)
    outgoing_keys = jnp.einsum(
        "wn,nki->wki", transfers, key_halfprec, preferred_element_type=jnp.float32
    ).astype(jnp.bfloat16)
    send_values = jnp.einsum(
        "wn,nki->wki", transfers, values, preferred_element_type=jnp.float32
    ).astype(jnp.bfloat16)
    got_keys, got_values = (
        lax.all_to_all(
            lax.all_to_all(outgoing_keys, "conv", split_axis=0, concat_axis=0, tiled=True),
            "tensor",
            split_axis=2,
            concat_axis=1,
            tiled=True,
        ),
        lax.all_to_all(
            lax.all_to_all(send_values, "conv", split_axis=0, concat_axis=0, tiled=True),
            "tensor",
            split_axis=2,
            concat_axis=1,
            tiled=True,
        ),
    )
    tile_keys = jnp.einsum(
        "to,orf->rtf", takes, got_keys, preferred_element_type=jnp.float32
    ).astype(jnp.bfloat16)
    tile_values = jnp.einsum(
        "to,orf->rtf", takes, got_values, preferred_element_type=jnp.float32
    ).astype(jnp.bfloat16)
    query_raw = queries[0].astype(jnp.float32).reshape(token_count, query_heads, head_size)
    query_normed, query_back = jax.vjp(lambda inputs: head_norm(inputs, q_gain), query_raw)
    query_bf = query_normed.astype(jnp.bfloat16).reshape(
        token_count, kv_local, group_size, head_size
    )
    grad_bf = (
        (gate_value * d_out[0].astype(jnp.float32))
        .astype(jnp.bfloat16)
        .reshape(token_count, kv_local, group_size, head_size)
    )
    own_start = sequence_index * token_count
    all_queries = lax.all_gather(query_bf, "seq", axis=0, tiled=True)
    all_grads = lax.all_gather(grad_bf, "seq", axis=0, tiled=True)
    share_rows = tile_keys.shape[0]
    row_start = sequence_index * share_rows
    part_sum, part_weighted = attend_forward(
        all_queries, tile_keys, tile_values, seen_all, row_start, score_scale
    )
    all_weighted, all_weight_sum = (
        lax.psum(part_weighted.astype(jnp.bfloat16), "seq").astype(jnp.float32),
        lax.psum(part_sum.astype(jnp.bfloat16), "seq").astype(jnp.float32),
    )
    safe_all = jnp.where(all_weight_sum > 0, all_weight_sum, 1.0)
    context_all = all_weighted / jnp.transpose(safe_all, (2, 0, 1))[..., None]
    context = lax.dynamic_slice_in_dim(context_all, own_start, token_count, 0)
    row_delta = jnp.transpose(
        jnp.sum(all_grads.astype(jnp.float32) * context_all, axis=-1), (1, 2, 0)
    )
    grad_part, key_sums, value_sums = attend_backward(
        all_queries,
        all_grads,
        tile_keys,
        tile_values,
        seen_all,
        row_start,
        safe_all,
        row_delta,
        score_scale,
        token_count,
    )
    grad_query = lax.psum_scatter(
        grad_part.astype(jnp.bfloat16), "seq", scatter_dimension=0, tiled=True
    ).astype(jnp.float32)
    attended = (
        (gate_value * context).astype(jnp.bfloat16).reshape(1, token_count, query_heads * head_size)
    )
    key_round = key_sums.astype(jnp.bfloat16)
    value_round = value_sums.astype(jnp.bfloat16)
    back_keys = jnp.einsum(
        "to,rtf->orf", takes, key_round, preferred_element_type=jnp.float32
    ).astype(jnp.bfloat16)
    back_values = jnp.einsum(
        "to,rtf->orf", takes, value_round, preferred_element_type=jnp.float32
    ).astype(jnp.bfloat16)
    returned_keys, returned_values = (
        lax.all_to_all(
            lax.all_to_all(back_keys, "conv", split_axis=0, concat_axis=0, tiled=True),
            "tensor",
            split_axis=1,
            concat_axis=2,
            tiled=True,
        ),
        lax.all_to_all(
            lax.all_to_all(back_values, "conv", split_axis=0, concat_axis=0, tiled=True),
            "tensor",
            split_axis=1,
            concat_axis=2,
            tiled=True,
        ),
    )
    positioned_keys = jnp.einsum(
        "ew,eig->wig", transfers, returned_keys, preferred_element_type=jnp.float32
    )
    d_values = jnp.einsum(
        "ew,eig->wig", transfers, returned_values, preferred_element_type=jnp.float32
    ).astype(jnp.bfloat16)
    d_keys = key_back(positioned_keys.reshape(slot_count, row_local, kv_heads, head_size))[0]
    d_keys = d_keys.astype(jnp.bfloat16).reshape(slot_count, row_local, features)
    d_queries = query_back(grad_query.reshape(token_count, query_heads, head_size))[0]
    d_queries = d_queries.astype(jnp.bfloat16).reshape(1, token_count, query_heads * head_size)
    return (attended, d_queries, d_keys, d_values)


LOG2E = math.log2(math.e)


def row_chunks(rows):
    starts = list(range(0, max(rows - 511, 1), 512))
    return [(a, b - a) for a, b in zip(starts, starts[1:] + [rows])]


def inverse_rms(inputs):
    return lax.rsqrt(jnp.mean(inputs * inputs, axis=-1, keepdims=True) + EPSILON)


def norm_back(inputs, inv, gained):
    return inv * gained - inputs * (inv * inv * inv) * jnp.mean(
        inputs * gained, axis=-1, keepdims=True
    )


def dot(lhs, rhs):
    return jnp.dot(lhs, rhs, preferred_element_type=jnp.float32)


def prepare_tile(tile, k_raw, v_raw, k_gain, kn, kt, vt):
    rows = k_raw.shape[1]
    for start in range(0, rows, 128):
        at = pl.ds(start, 128)
        raw = k_raw[tile, at, :].astype(jnp.float32)
        normed = raw * inverse_rms(raw) * k_gain
        kn[tile, at, :] = normed.astype(jnp.bfloat16)
        kt[tile, :, at] = normed.T.astype(jnp.bfloat16)
        vt[tile, :, at] = v_raw[tile, at, :].astype(jnp.float32).T.astype(jnp.bfloat16)


def finish_tile(tile, k_raw, k_gain, dk, dv, dk_out, dv_out):
    rows = k_raw.shape[1]
    for start in range(0, rows, 128):
        at = pl.ds(start, 128)
        raw = k_raw[tile, at, :].astype(jnp.float32)
        grad = dk[tile, at, :] * (1.0 / LOG2E) * k_gain
        dk_out[tile, at, :] = norm_back(raw, inverse_rms(raw), grad).astype(jnp.bfloat16)
        dv_out[tile, at, :] = dv[tile, at, :].astype(jnp.bfloat16)


def attend_block(
    block, last_seen, tiles, q_raw, d_out, seen, gate_value, q_gain, v_raw, kn, kt, vt,
    att_out, dq_out, wts, qs, qst, dos, dost, acc, total, dqt, dk, dv,
):
    size = q_gain.shape[1]
    group = q_raw.shape[1] // size
    count = seen.shape[2] // group
    rows = v_raw.shape[1]
    chunks = row_chunks(rows)
    scale = 1.0 / math.sqrt(size)
    at = pl.ds(pl.multiple_of(block * count, count), count)
    for g in range(group):
        raw = q_raw[at, pl.ds(g * size, size)].astype(jnp.float32)
        normed = raw * inverse_rms(raw) * (q_gain * (scale * LOG2E))
        qs[pl.ds(g * count, count), :] = normed.astype(jnp.bfloat16)
        qst[:, pl.ds(g * count, count)] = normed.T.astype(jnp.bfloat16)
    seen_row = seen[block]
    acc[...] = jnp.zeros_like(acc)
    total[...] = jnp.zeros_like(total)
    dqt[...] = jnp.zeros_like(dqt)

    for tile in range(tiles):
        @pl.when(last_seen > tile)
        def _(tile=tile):
            mask = (seen_row > tile).astype(jnp.float32)
            part = jnp.zeros(acc.shape, jnp.float32)
            part_sum = jnp.zeros(total.shape, jnp.float32)
            for start, length in chunks:
                here = pl.ds(start, length)
                w = jnp.exp2(dot(kn[tile, here, :], qst[...]))
                if start + length > TILE:
                    ids = start + lax.broadcasted_iota(jnp.int32, w.shape, 0)
                    w = jnp.where(ids < TILE, w, 0.0)
                part_sum = part_sum + jnp.sum(w, axis=0, keepdims=True)
                w_bf = w.astype(jnp.bfloat16)
                wts[tile, here, :] = w_bf
                part = part + dot(vt[tile, :, here], w_bf)
            acc[...] += part * mask
            total[...] += part_sum * mask

    safe = jnp.where(total[...] > 0, total[...], 1.0)
    inv = 1.0 / safe
    ctx = acc[...] * inv
    for g in range(group):
        lanes = pl.ds(g * count, count)
        grad = d_out[at, pl.ds(g * size, size)].astype(jnp.float32) * gate_value
        dost[:, lanes] = grad.T
        att_out[at, pl.ds(g * size, size)] = (
            (gate_value * ctx[:, g * count:(g + 1) * count]).T.astype(jnp.bfloat16)
        )
    scaled = (dost[...] * inv).astype(jnp.bfloat16)
    scaled32 = scaled.astype(jnp.float32)
    delta = jnp.sum(scaled32 * ctx, axis=0, keepdims=True)

    for tile in range(tiles):
        @pl.when(last_seen > tile)
        def _(tile=tile):
            mask = (seen_row > tile).astype(jnp.float32)
            cut32 = scaled32 * mask
            cut = cut32.astype(jnp.bfloat16)
            for g in range(group):
                dos[pl.ds(g * count, count), :] = (
                    cut32[:, g * count:(g + 1) * count].T.astype(jnp.bfloat16)
                )
            low = delta * mask
            part = jnp.zeros(dqt.shape, jnp.float32)
            for start, length in chunks:
                here = pl.ds(start, length)
                w_bf = wts[tile, here, :]
                dp = dot(v_raw[tile, here, :], cut)
                ds = (w_bf.astype(jnp.float32) * (dp - low)).astype(jnp.bfloat16)
                dv[tile, here, :] += dot(w_bf, dos[...])
                dk[tile, here, :] += dot(ds, qs[...])
                part = part + dot(kt[tile, :, here], ds)
            dqt[...] += part

    for g in range(group):
        raw = q_raw[at, pl.ds(g * size, size)].astype(jnp.float32)
        grad = dqt[:, pl.ds(g * count, count)].T * (q_gain * scale)
        dq_out[at, pl.ds(g * size, size)] = norm_back(raw, inverse_rms(raw), grad).astype(
            jnp.bfloat16
        )


def head_kernel(
    last, counts, gate, q_raw, d_out, k_raw, v_raw, seen, q_gain_ref, k_gain_ref,
    att_out, dq_out, dk_out, dv_out,
    kn, kt, vt, wts, qs, qst, dos, dost, acc, total, dqt, dk, dv,
):
    tiles = k_raw.shape[0]
    q_gain = q_gain_ref[...]
    k_gain = k_gain_ref[...]
    dk[...] = jnp.zeros_like(dk)
    dv[...] = jnp.zeros_like(dv)
    for tile in range(tiles):
        prepare_tile(tile, k_raw, v_raw, k_gain, kn, kt, vt)

    @pl.loop(0, seen.shape[0])
    def _(block):
        attend_block(
            block, last[block], tiles, q_raw, d_out, seen, gate[0], q_gain, v_raw, kn, kt, vt,
            att_out, dq_out, wts, qs, qst, dos, dost, acc, total, dqt, dk, dv,
        )

    for tile in range(tiles):
        finish_tile(tile, k_raw, k_gain, dk, dv, dk_out, dv_out)


def core_scratch(tiles, rows, size, lanes):
    bf, f32 = jnp.bfloat16, jnp.float32
    return [
        pltpu.VMEM((tiles, rows, size), bf),
        pltpu.VMEM((tiles, size, rows), bf),
        pltpu.VMEM((tiles, size, rows), bf),
        pltpu.VMEM((tiles, rows, lanes), bf),
        pltpu.VMEM((lanes, size), bf),
        pltpu.VMEM((size, lanes), bf),
        pltpu.VMEM((lanes, size), bf),
        pltpu.VMEM((size, lanes), f32),
        pltpu.VMEM((size, lanes), f32),
        pltpu.VMEM((1, lanes), f32),
        pltpu.VMEM((size, lanes), f32),
        pltpu.VMEM((tiles, rows, size), f32),
        pltpu.VMEM((tiles, rows, size), f32),
    ]


def move_convs(outgoing):
    count = len(outgoing)
    return [outgoing[0]] + [
        lax.ppermute(outgoing[shift], "conv", [(i, (i + shift) % count) for i in range(count)])
        for shift in range(1, count)
    ]


def choose(arrived, index):
    chosen = arrived[0]
    for shift in range(1, len(arrived)):
        chosen = jnp.where(index == shift, arrived[shift], chosen)
    return chosen


def head_shards(queries, keys, values, q_gain, k_gain, gate, tile_count, tile_owner, visible, d_out):
    conv_count = lax.axis_size("conv")
    tensor_count = lax.axis_size("tensor")
    seq_count = lax.axis_size("seq")
    conv_index = lax.axis_index("conv")
    slot_count, row_local, features = keys.shape
    size = q_gain.shape[0]
    block_tokens, width = queries.shape[1:]
    group = width // (features // tensor_count)
    lanes = group * block_tokens
    everyone = ("conv", "seq", "tensor")

    own_owners = lax.dynamic_index_in_dim(tile_owner, conv_index, 0, keepdims=False)
    own_count = lax.dynamic_index_in_dim(tile_count, conv_index, 0, keepdims=False)
    seen = jnp.minimum(lax.dynamic_index_in_dim(visible, conv_index, 0, keepdims=False), own_count)
    seen = seen.reshape(seq_count, 1, block_tokens)
    last = seen[:, 0, -1]
    seen = jnp.tile(seen, (1, 1, group))

    both = jnp.stack([queries[0], d_out[0]]).reshape(2, block_tokens, seq_count, width // seq_count)
    both = lax.all_to_all(both, "seq", split_axis=2, concat_axis=1, tiled=True)
    both = both.reshape(2, seq_count * block_tokens, width // seq_count)

    goes = tile_owner == conv_index
    slot_of = jnp.argmax(goes, axis=1)
    shifts = list(range(conv_count))
    own_shift = jnp.remainder(conv_index - own_owners, conv_count)

    def fetch(stored):
        outgoing = [
            lax.dynamic_index_in_dim(
                stored, slot_of[jnp.remainder(conv_index + shift, conv_count)], 0, keepdims=False
            )
            for shift in shifts
        ]
        arrived = move_convs(outgoing)
        mine = jnp.stack([choose(arrived, own_shift[tile]) for tile in range(slot_count)])
        mine = mine.reshape(slot_count, row_local, tensor_count, seq_count, size)
        mine = jnp.transpose(mine, (3, 2, 0, 1, 4)).reshape(-1, slot_count, row_local, size)
        mine = lax.all_to_all(mine, ("seq", "tensor"), split_axis=0, concat_axis=0, tiled=True)
        return jnp.transpose(mine, (1, 0, 2, 3)).reshape(slot_count, -1, size)

    key_tiles = fetch(keys)
    value_tiles = fetch(values)
    rows = key_tiles.shape[1]

    vmem = pl.BlockSpec(memory_space=pltpu.VMEM)
    smem = pl.BlockSpec(memory_space=pltpu.SMEM)
    att, dq, dk, dv = pl.pallas_call(
        head_kernel,
        out_shape=[jax.ShapeDtypeStruct(both.shape[1:], jnp.bfloat16)] * 2
        + [jax.ShapeDtypeStruct((slot_count, rows, size), jnp.bfloat16)] * 2,
        in_specs=[smem] * 3 + [vmem] * 7,
        out_specs=[vmem] * 4,
        scratch_shapes=core_scratch(slot_count, rows, size, lanes),
        compiler_params=pltpu.CompilerParams(vmem_limit_bytes=60 << 20),
    )(
        last, own_count.reshape(1), jnp.tanh(gate), both[0], both[1], key_tiles, value_tiles,
        seen, q_gain[None], k_gain[None],
    )

    tile_of = jnp.argmax(own_owners[None, :] == jnp.arange(conv_count)[:, None], axis=1)
    taker = jnp.argmax(goes, axis=0)
    used = jnp.any(goes, axis=0)
    taker_shift = jnp.remainder(conv_index - taker, conv_count)

    def give_back(grads):
        grads = jnp.transpose(grads.reshape(slot_count, -1, row_local, size), (1, 0, 2, 3))
        grads = lax.all_to_all(grads, ("seq", "tensor"), split_axis=0, concat_axis=0, tiled=True)
        grads = grads.reshape(seq_count, tensor_count, slot_count, row_local, size)
        grads = jnp.transpose(grads, (2, 3, 1, 0, 4)).reshape(slot_count, row_local, features)
        outgoing = [
            lax.dynamic_index_in_dim(
                grads, tile_of[jnp.remainder(conv_index + shift, conv_count)], 0, keepdims=False
            )
            for shift in shifts
        ]
        arrived = move_convs(outgoing)
        zero = jnp.zeros((), jnp.bfloat16)
        return jnp.stack(
            [
                jnp.where(used[slot], choose(arrived, taker_shift[slot]), zero)
                for slot in range(slot_count)
            ]
        )

    d_keys = give_back(dk)
    outs = jnp.stack([att, dq])
    outs, d_keys = lax.optimization_barrier((outs, d_keys))
    outs = outs.reshape(2, seq_count, block_tokens, width // seq_count)
    outs = lax.all_to_all(outs, "seq", split_axis=1, concat_axis=3, tiled=True)
    attended = outs[0].reshape(1, block_tokens, width)
    d_queries = outs[1].reshape(1, block_tokens, width)

    return (attended, d_queries, d_keys, give_back(dv))


def shards(queries, keys, *rest):
    heads = keys.shape[2] // rest[1].shape[0]
    split = lax.axis_size("seq") * lax.axis_size("tensor")
    return (head_shards if heads == split else row_shards)(queries, keys, *rest)


def solution(mesh):
    in_specs = (
        P("conv", "seq", "tensor"),
        P("conv", ("seq", "tensor"), None),
        P("conv", ("seq", "tensor"), None),
        P(),
        P(),
        P(),
        P(),
        P(),
        P(),
        P("conv", "seq", "tensor"),
    )
    out_specs = (
        P("conv", "seq", "tensor"),
        P("conv", "seq", "tensor"),
        P("conv", ("seq", "tensor"), None),
        P("conv", ("seq", "tensor"), None),
    )
    return jax.shard_map(shards, mesh=mesh, in_specs=in_specs, out_specs=out_specs, check_vma=False)
```
